256 devices in a mesh: freq: 16 (over x, y), space: 16 (over z, core).
Axes of the slice: x: 4, y: 4, z: 8, core: 2. Of those that a mesh axis runs over, the one named last changes fastest.
Arguments:
- spectra: bfloat16 [2, 256, 24, 65536], P(None, 'freq', None, 'space'), may hold values from -6 to 6
- eigvecs: bfloat16 [2, 256, 4, 65536], P(None, 'freq', None, 'space'), may hold values from -6 to 6
- weights: bfloat16 [65536], P('space'), may hold values from 0.19921875 to 5
Outputs:
- filtered: float32 [3200, 65536], P(None, ('space', 'freq'))
The draws below stay inside these ranges and needn't reach their ends.
All inputs are finite; a program needn't handle non-finite values.
Results may differ from the reference program's by a relative error of at most 0.004.
Values may be sent and summed in bfloat16 or wider, within the bound.
No kernel may reach another device: no remote copies, remote signals or barrier semaphores. Data moves between devices by JAX's collectives and lax.ppermute only.
A program may use at most 64 MiB of HBM per device.

```python
import math
import jax
import jax.numpy as jnp
from jax import lax

NFREQ = 256
MODES = 4
BLOCKS = 24
P_DEV = 4096
POINTS = 65536
TIME = 3200
N_SPACE = 16


def level_of(rng, shape, split, smallest, top_value):
    factor_of, own = 1.0, jax.random.fold_in(rng, 6)
    for position, parts in split:
        heights = jnp.exp(jax.random.uniform(jax.random.fold_in(own, position), (parts,), jnp.float32, smallest / len(split), top_value / len(split)))
        factor_of = factor_of * jnp.repeat(heights, shape[position] // parts).reshape([-1 if axis == position else 1 for axis in range(len(shape))])
    return factor_of


def gaussian(rng, extent, deviation, limit, split=(), kind=jnp.bfloat16):
    drawn = deviation * jax.random.normal(rng, extent, jnp.float32)
    if split:
        drawn = drawn * level_of(rng, extent, split, -0.22, 0.18)
    return jnp.clip(drawn, -limit, limit).astype(kind)


def setup_inputs(seed: int = 0) -> dict:
    splits = jax.random.split(jax.random.key(seed), 4)
    spectra = gaussian(splits[0], (2, NFREQ, BLOCKS, POINTS), 1.0, 6.0, ((1, 16), (3, 16)))
    eigvecs = gaussian(splits[1], (2, NFREQ, MODES, POINTS), 1.0, 6.0, ((1, 16), (3, 16)))
    weights = jnp.clip(jnp.exp(math.log(5.0) - 3.2227897 * jax.random.uniform(splits[2], (POINTS,), jnp.float32) ** level_of(splits[2], (POINTS,), ((0, 16),), -0.2, 0.2)), 0.19921875, 5.0).astype(jnp.bfloat16)
    return dict(spectra=spectra, eigvecs=eigvecs, weights=weights)


def coefficient_terms(spectra_block, weighted_block):
    spectra_real = spectra_block[0].astype(jnp.float32)
    spectra_imag = spectra_block[1].astype(jnp.float32)
    modes_real = weighted_block[0].astype(jnp.float32)
    modes_imag = weighted_block[1].astype(jnp.float32)
    highest = lax.Precision.HIGHEST
    real_terms = jnp.einsum('kmp,kbp->kbm', modes_real, spectra_real, precision=highest) + jnp.einsum('kmp,kbp->kbm', modes_imag, spectra_imag, precision=highest)
    imag_terms = jnp.einsum('kmp,kbp->kbm', modes_real, spectra_imag, precision=highest) - jnp.einsum('kmp,kbp->kbm', modes_imag, spectra_real, precision=highest)
    return jnp.stack([real_terms, imag_terms])

def rebuild(modes_block, coefficients):
    highest = lax.Precision.HIGHEST
    modes_real = modes_block[0].astype(jnp.float32)
    modes_imag = modes_block[1].astype(jnp.float32)
    coef_real = coefficients[0]
    coef_imag = coefficients[1]
    real_part = jnp.einsum('kmp,kbm->kbp', modes_real, coef_real, precision=highest) - jnp.einsum('kmp,kbm->kbp', modes_imag, coef_imag, precision=highest)
    imag_part = jnp.einsum('kmp,kbm->kbp', modes_real, coef_imag, precision=highest) + jnp.einsum('kmp,kbm->kbp', modes_imag, coef_real, precision=highest)
    return jnp.stack([real_part, imag_part]).astype(jnp.bfloat16)

def correlation_add(series):
    length = series.shape[0]
    half_length = length // 2
    window = jnp.sin(math.pi * (jnp.arange(length, dtype=jnp.float32) + 0.5) / length)
    shaped = (series * window[:, None, None]).reshape(2, half_length, series.shape[1], series.shape[2])
    zeros_block = jnp.zeros((half_length, 1, series.shape[2]), jnp.float32)
    leading = jnp.concatenate([shaped[0], zeros_block], axis=1)
    trailing = jnp.concatenate([zeros_block, shaped[1]], axis=1)
    summed = leading + trailing
    return jnp.transpose(summed, (1, 0, 2)).reshape(-1, series.shape[2])

def reference(spectra, eigvecs, weights):
    weighted = (eigvecs.astype(jnp.float32) * weights.astype(jnp.float32)).astype(jnp.bfloat16)
    factor = 1.0 / math.sqrt(POINTS)

    def partial_sum(index):
        start = (index * P_DEV).astype(jnp.int32)
        return coefficient_terms(lax.dynamic_slice_in_dim(spectra, start, P_DEV, 3), lax.dynamic_slice_in_dim(weighted, start, P_DEV, 3))
    indices = jnp.arange(N_SPACE, dtype=jnp.int32)
    coefficients = lax.optimization_barrier(jnp.sum(lax.map(partial_sum, indices), axis=0)) * factor

    def filtered_block(index):
        start = (index * P_DEV).astype(jnp.int32)
        rebuilt = rebuild(lax.dynamic_slice_in_dim(eigvecs, start, P_DEV, 3), coefficients).astype(jnp.float32)
        series = jnp.fft.ifft(rebuilt[0] + 1j * rebuilt[1], axis=0).real * math.sqrt(NFREQ)
        return correlation_add(series)
    pieces = lax.map(filtered_block, indices)
    return jnp.transpose(pieces, (1, 0, 2)).reshape(TIME, POINTS)
```

```python
import math

import jax
import jax.numpy as jnp
import numpy as np
from jax import lax
from jax.experimental import pallas as pl
from jax.experimental.pallas import tpu as pltpu
from jax.sharding import PartitionSpec as P

VMEM_LIMIT = 48 * 1024 * 1024


def cut_points(eigvecs, parts):
    width = eigvecs.shape[3] // parts

    def kernel(source, pieces, done):
        copies = []
        for part in range(parts):
            columns = source.at[:, :, :, pl.ds(part * width, width)]
            copies.append(pltpu.make_async_copy(columns, pieces.at[part], done.at[part]))
        for copy in copies:
            copy.start()
        for copy in copies:
            copy.wait()

    return pl.pallas_call(
        kernel,
        out_shape=jax.ShapeDtypeStruct((parts, *eigvecs.shape[:3], width), eigvecs.dtype),
        in_specs=[pl.BlockSpec(memory_space=pl.ANY)],
        out_specs=pl.BlockSpec(memory_space=pl.ANY),
        scratch_shapes=[pltpu.SemaphoreType.DMA((parts,))],
        cost_estimate=pl.CostEstimate(
            flops=0, transcendentals=0, bytes_accessed=2 * eigvecs.size * eigvecs.dtype.itemsize
        ),
        name="cut_points",
    )(eigvecs)


def project(spectra, eigvecs, weights, per_step):
    _, freqs, blocks, points = spectra.shape
    modes = eigvecs.shape[2]
    half = freqs * modes
    steps = freqs // per_step

    def kernel(spectra_ref, eigvecs_ref, weights_ref, out_ref, terms):
        step = pl.program_id(0)

        @pl.when(step == 0)
        def _():
            terms[...] = jnp.zeros_like(terms)

        scale = weights_ref[...].astype(jnp.float32)
        rows = per_step * modes
        pieces = [[[], []], [[], []]]
        for k in range(per_step):
            weighted = jnp.concatenate(
                [
                    (eigvecs_ref[part, k].astype(jnp.float32) * scale).astype(jnp.bfloat16)
                    for part in range(2)
                ],
                axis=0,
            )
            for part in range(2):
                product = lax.dot_general(
                    weighted,
                    spectra_ref[part, k],
                    (((1,), (1,)), ((), ())),
                    preferred_element_type=jnp.float32,
                )
                for kind in range(2):
                    pieces[part][kind].append(product[kind * modes : (kind + 1) * modes])
        for part in range(2):
            for kind in range(2):
                first = pl.multiple_of(kind * half + step * rows, 8)
                terms[part, pl.ds(first, rows), :blocks] = jnp.concatenate(
                    pieces[part][kind], axis=0
                )

        @pl.when(step == steps - 1)
        def _():
            of_real = jnp.transpose(terms[0])[:blocks]
            of_imag = pltpu.roll(jnp.transpose(terms[1])[:blocks], half, 1)
            lane = lax.broadcasted_iota(jnp.int32, of_real.shape, 1)
            out_ref[...] = jnp.where(lane < half, of_real, -of_real) + of_imag

    return pl.pallas_call(
        kernel,
        grid=(steps,),
        out_shape=jax.ShapeDtypeStruct((blocks, 2 * half), jnp.float32),
        in_specs=[
            pl.BlockSpec((2, per_step, blocks, points), lambda i: (0, i, 0, 0)),
            pl.BlockSpec((2, per_step, modes, points), lambda i: (0, i, 0, 0)),
            pl.BlockSpec((1, points), lambda i: (0, 0)),
        ],
        out_specs=pl.BlockSpec((blocks, 2 * half), lambda i: (0, 0)),
        scratch_shapes=[pltpu.VMEM((2, 2 * half, 2 * half), jnp.float32)],
        compiler_params=pltpu.CompilerParams(vmem_limit_bytes=VMEM_LIMIT),
        cost_estimate=pl.CostEstimate(
            flops=8 * freqs * blocks * modes * points,
            transcendentals=0,
            bytes_accessed=2 * (spectra.size + eigvecs.size),
        ),
        name="project",
    )(spectra, eigvecs, weights.reshape(1, points))


def transform_table(length, groups):
    sample = np.arange(length)
    phase = 2.0 * np.pi * ((sample[:, None] * sample[None, :]) % length) / length
    window = np.sin(np.pi * (sample + 0.5) / length) / math.sqrt(length)
    table = np.stack([np.cos(phase), -np.sin(phase)], axis=1) * window[:, None, None]
    table = table.reshape(length, 2, groups, length // groups).transpose(0, 2, 1, 3)
    return jnp.asarray(table.reshape(length, 2 * length), jnp.bfloat16)


def synthesize(coefficients, moved_modes, table):
    groups, blocks, lanes = coefficients.shape
    columns = moved_modes.shape[2]
    length = table.shape[0]
    freqs = length // groups
    modes = lanes // (2 * freqs)
    half_lanes = lanes // 2
    half = length // 2

    def kernel(coef_ref, modes_ref, table_ref, out_ref, high, low, rebuilt, result, done):
        lane = lax.broadcasted_iota(jnp.int32, (freqs, lanes), 1)
        row = lax.broadcasted_iota(jnp.int32, (freqs, lanes), 0)
        own = jnp.where((lane % half_lanes) // modes == row, 1.0, 0.0)
        signed = jnp.where(lane < half_lanes, own, -own)
        for group in range(groups):
            plain = coef_ref[group]
            for kind, value in enumerate((plain, pltpu.roll(plain, half_lanes, 1))):
                rounded = value.astype(jnp.bfloat16).astype(jnp.float32)
                high[kind, group] = rounded
                low[kind, group] = value - rounded
        for group in range(groups):
            tiles = []
            for block in range(blocks):
                for kind, mask in enumerate((signed, own)):
                    tiles.append(
                        jnp.concatenate(
                            [
                                (jnp.broadcast_to(
                                    side[kind, group, pl.ds(block, 1), :], (freqs, lanes)
                                ) * mask).astype(jnp.bfloat16)
                                for side in (high, low)
                            ],
                            axis=1,
                        )
                    )
            values = modes_ref[group]
            product = jnp.dot(
                jnp.concatenate(tiles, axis=0),
                jnp.concatenate([values, values], axis=0),
                preferred_element_type=jnp.float32,
            )
            rebuilt[:, group * 2 * freqs : (group + 1) * 2 * freqs, :] = product.astype(
                jnp.bfloat16
            ).reshape(blocks, 2 * freqs, columns)
        result[0] = jnp.zeros((half, columns), jnp.float32)

        def send(block):
            return pltpu.make_async_copy(result.at[block], out_ref.at[block], done.at[block])

        for block in range(blocks):
            series = jnp.dot(table_ref[...], rebuilt[block], preferred_element_type=jnp.float32)
            result[block] += series[:half]
            result[block + 1] = series[half:]
            send(block).start()
        send(blocks).start()
        for block in range(blocks + 1):
            send(block).wait()

    return pl.pallas_call(
        kernel,
        out_shape=jax.ShapeDtypeStruct((blocks + 1, half, columns), jnp.float32),
        in_specs=[pl.BlockSpec(memory_space=pltpu.VMEM)] * 3,
        out_specs=pl.BlockSpec(memory_space=pl.ANY),
        scratch_shapes=[
            pltpu.VMEM((2, groups, blocks, lanes), jnp.float32),
            pltpu.VMEM((2, groups, blocks, lanes), jnp.float32),
            pltpu.VMEM((blocks, 2 * length, columns), jnp.bfloat16),
            pltpu.VMEM((blocks + 1, half, columns), jnp.float32),
            pltpu.SemaphoreType.DMA((blocks + 1,)),
        ],
        compiler_params=pltpu.CompilerParams(vmem_limit_bytes=VMEM_LIMIT),
        cost_estimate=pl.CostEstimate(
            flops=4 * length * length * blocks * columns,
            transcendentals=0,
            bytes_accessed=4 * (blocks + 1) * half * columns,
        ),
        name="synthesize",
    )(coefficients, moved_modes, table)


def sum_over_space(partial):
    count = lax.axis_size("space")
    chips = count // 2

    def beside(value):
        return lax.ppermute(value, "space", [(i, i ^ 1) for i in range(count)])

    def around(value, hops):
        pairs = [(2 * z, 2 * ((z + hops) % chips)) for z in range(chips)]
        if 2 * hops != chips:
            pairs += [(2 * z + 1, 2 * ((z - hops) % chips) + 1) for z in range(chips)]
        return lax.ppermute(value, "space", pairs)

    chip = partial + beside(partial)
    arrived = sum(around(chip, hops) for hops in range(1, chips // 2 + 1))
    return chip + arrived + beside(arrived)


def body(spectra, eigvecs, weights):
    points_dev = spectra.shape[3]
    groups = lax.axis_size("freq")
    factor = 1.0 / math.sqrt(points_dev * lax.axis_size("space"))
    pieces = cut_points(eigvecs, groups)
    moved = lax.all_to_all(pieces, "freq", split_axis=0, concat_axis=0, tiled=True)
    same_eigvecs, _ = lax.optimization_barrier((eigvecs, pieces))
    coefficients = sum_over_space(project(spectra, same_eigvecs, weights, 4)) * factor
    coefficients, moved = lax.optimization_barrier((coefficients, moved))
    copies = jnp.broadcast_to(coefficients, (groups, *coefficients.shape))
    gathered = lax.all_to_all(copies, "freq", split_axis=0, concat_axis=0, tiled=True)
    length = groups * spectra.shape[1]
    filtered = synthesize(
        gathered,
        moved.reshape(groups, -1, moved.shape[-1]),
        transform_table(length, groups),
    )
    return filtered.reshape(-1, filtered.shape[-1])


def solution(mesh):
    placed = (P(None, "freq", None, "space"), P(None, "freq", None, "space"), P("space"))
    return jax.shard_map(
        body, mesh=mesh, in_specs=placed, out_specs=P(None, ("space", "freq")), check_vma=False
    )
```

```python
import math

import jax
import jax.numpy as jnp
import numpy as np
from jax import lax
from jax.experimental import pallas as pl
from jax.experimental.pallas import tpu as pltpu
from jax.sharding import PartitionSpec as P

MIB = 1024 * 1024
LANES = 128


def project(spectra, eigvecs, weights, copies):
    _, freqs, blocks, points = spectra.shape
    modes = eigvecs.shape[2]
    half = freqs * modes
    rows = 2 * freqs * blocks
    ends = [rows // 4, rows // 2, rows * 3 // 4, rows * 7 // 8, rows]
    starts = [0, *ends[:-1]]
    dtype = spectra.dtype

    def kernel(
        spectra_hbm, eigvecs_hbm, weights_hbm, out_ref,
        spectra_ref, eigvecs_ref, weights_ref, weighted, columns, total, done,
    ):
        small = pltpu.make_async_copy(weights_hbm, weights_ref, done.at[0])
        small.start()
        by_part = [
            pltpu.make_async_copy(eigvecs_hbm.at[part], eigvecs_ref.at[part], done.at[1 + part])
            for part in range(2)
        ]
        for copy in by_part:
            copy.start()
        by_rows = []
        for i, (start, end) in enumerate(zip(starts, ends)):
            some = pl.ds(start, end - start)
            by_rows.append(
                pltpu.make_async_copy(spectra_hbm.at[some], spectra_ref.at[some], done.at[3 + i])
            )
            by_rows[-1].start()
        small.wait()
        per_row = weights_ref[...].astype(jnp.float32)
        scale = jnp.concatenate([per_row[i : i + 1] for i in range(points // LANES)], axis=1)
        for part in range(2):
            by_part[part].wait()
            for k in range(freqs):
                first = part * half + k * modes
                weighted[first : first + modes] = (
                    eigvecs_ref[part, k].astype(jnp.float32) * scale
                )
        columns[...] = jnp.transpose(weighted[...]).astype(dtype)
        for copy, start, end in zip(by_rows, starts, ends):
            copy.wait()
            total[start:end] = jnp.dot(
                spectra_ref[start:end], columns[...], preferred_element_type=jnp.float32
            )
        lane = lax.broadcasted_iota(jnp.int32, (blocks, 2 * half), 1)
        sums = []
        for part in range(2):
            kept = jnp.zeros((blocks, 2 * half), jnp.float32)
            for k in range(freqs):
                first = (part * freqs + k) * blocks
                own = (lane % half) // modes == k
                kept = jnp.where(own, total[first : first + blocks], kept)
            sums.append(kept)
        value = jnp.where(lane < half, sums[0], -sums[0]) + pltpu.roll(sums[1], half, 1)
        for copy in range(copies):
            out_ref[copy] = value

    return pl.pallas_call(
        kernel,
        out_shape=jax.ShapeDtypeStruct((copies, blocks, 2 * half), jnp.float32),
        in_specs=[pl.BlockSpec(memory_space=pl.ANY)] * 3,
        out_specs=pl.BlockSpec(memory_space=pltpu.VMEM),
        scratch_shapes=[
            pltpu.VMEM((rows, points), dtype),
            pltpu.VMEM(eigvecs.shape, dtype),
            pltpu.VMEM((points // LANES, LANES), dtype),
            pltpu.VMEM((2 * half, points), jnp.float32),
            pltpu.VMEM((points, 2 * half), dtype),
            pltpu.VMEM((rows, 2 * half), jnp.float32),
            pltpu.SemaphoreType.DMA((3 + len(ends),)),
        ],
        compiler_params=pltpu.CompilerParams(vmem_limit_bytes=60 * MIB),
        cost_estimate=pl.CostEstimate(
            flops=8 * freqs * blocks * modes * points,
            transcendentals=0,
            bytes_accessed=2 * (spectra.size + eigvecs.size),
        ),
        name="project",
    )(spectra.reshape(rows, points), eigvecs, weights.reshape(points // LANES, LANES))


def cut_points(eigvecs, parts, spare):
    kinds, freqs, modes, points = eigvecs.shape
    width = points // parts
    rows = kinds * freqs * modes
    shape = (parts, rows + spare, width)

    def kernel(source, pieces, staged, done):
        copies = []
        for part in range(parts):
            for kind in range(kinds):
                for k in range(freqs):
                    first = (kind * freqs + k) * modes
                    staged[part, first : first + modes] = source[
                        kind, k, :, part * width : (part + 1) * width
                    ]
            copies.append(
                pltpu.make_async_copy(
                    staged.at[part], pieces.at[part, pl.ds(0, rows)], done.at[part]
                )
            )
            copies[-1].start()
        for copy in copies:
            copy.wait()

    return pl.pallas_call(
        kernel,
        out_shape=jax.ShapeDtypeStruct(shape, eigvecs.dtype),
        in_specs=[pl.BlockSpec(memory_space=pltpu.VMEM)],
        out_specs=pl.BlockSpec(memory_space=pl.ANY),
        scratch_shapes=[
            pltpu.VMEM((parts, rows, width), eigvecs.dtype),
            pltpu.SemaphoreType.DMA((parts,)),
        ],
        compiler_params=pltpu.CompilerParams(vmem_limit_bytes=8 * MIB),
        cost_estimate=pl.CostEstimate(
            flops=0, transcendentals=0, bytes_accessed=2 * eigvecs.size * eigvecs.dtype.itemsize
        ),
        name="cut_points",
    )(eigvecs)


def add_coefficients(terms, pieces, factor):
    _, blocks, lanes = terms.shape
    parts, rows, _ = pieces.shape

    def kernel(terms_ref, _, out_ref, staged, done):
        value = terms_ref[0]
        for i in range(1, terms.shape[0]):
            value += terms_ref[i]
        value *= factor
        high = value.astype(jnp.bfloat16)
        staged[:, :lanes] = high
        staged[:, lanes:] = (value - high.astype(jnp.float32)).astype(jnp.bfloat16)
        copies = [
            pltpu.make_async_copy(
                staged, out_ref.at[part, pl.ds(rows - blocks, blocks)], done.at[part]
            )
            for part in range(parts)
        ]
        for copy in copies:
            copy.start()
        for copy in copies:
            copy.wait()

    return pl.pallas_call(
        kernel,
        out_shape=jax.ShapeDtypeStruct(pieces.shape, pieces.dtype),
        in_specs=[pl.BlockSpec(memory_space=pltpu.VMEM), pl.BlockSpec(memory_space=pl.ANY)],
        out_specs=pl.BlockSpec(memory_space=pl.ANY),
        scratch_shapes=[
            pltpu.VMEM((blocks, 2 * lanes), pieces.dtype),
            pltpu.SemaphoreType.DMA((parts,)),
        ],
        input_output_aliases={1: 0},
        compiler_params=pltpu.CompilerParams(vmem_limit_bytes=4 * MIB),
        cost_estimate=pl.CostEstimate(
            flops=terms.size, transcendentals=0, bytes_accessed=4 * terms.size
        ),
        name="add_coefficients",
    )(terms, pieces)


def transform_table(length, groups):
    sample = np.arange(length)
    phase = 2.0 * np.pi * ((sample[:, None] * sample[None, :]) % length) / length
    window = np.sin(np.pi * (sample + 0.5) / length) / math.sqrt(length)
    table = np.stack([np.cos(phase), -np.sin(phase)], axis=1) * window[:, None, None]
    table = table.reshape(length, 2, groups, length // groups).transpose(0, 2, 1, 3)
    return jnp.asarray(table.reshape(length, 2 * length), jnp.bfloat16)


def synthesize(pieces, table, blocks):
    groups, rows, columns = pieces.shape
    lanes = rows - blocks
    length = table.shape[0]
    freqs = length // groups
    modes = lanes // (2 * freqs)
    half_lanes = lanes // 2
    half = length // 2

    def kernel(pieces_ref, table_ref, out_ref, high, low, rebuilt, result, done):
        lane = lax.broadcasted_iota(jnp.int32, (freqs, lanes), 1)
        row = lax.broadcasted_iota(jnp.int32, (freqs, lanes), 0)
        own = jnp.where((lane % half_lanes) // modes == row, 1.0, 0.0)
        signed = jnp.where(lane < half_lanes, own, -own)
        for group in range(groups):
            both = pieces_ref[group, lanes:].astype(jnp.float32)
            for side, value in ((high, both[:, :lanes]), (low, both[:, lanes:])):
                side[0, group] = value
                side[1, group] = pltpu.roll(value, half_lanes, 1)
        for group in range(groups):
            tiles = []
            for block in range(blocks):
                for kind, mask in enumerate((signed, own)):
                    tiles.append(
                        jnp.concatenate(
                            [
                                (jnp.broadcast_to(
                                    side[kind, group, pl.ds(block, 1), :], (freqs, lanes)
                                ) * mask).astype(jnp.bfloat16)
                                for side in (high, low)
                            ],
                            axis=1,
                        )
                    )
            values = pieces_ref[group, :lanes]
            product = jnp.dot(
                jnp.concatenate(tiles, axis=0),
                jnp.concatenate([values, values], axis=0),
                preferred_element_type=jnp.float32,
            )
            rebuilt[:, group * 2 * freqs : (group + 1) * 2 * freqs, :] = product.astype(
                jnp.bfloat16
            ).reshape(blocks, 2 * freqs, columns)
        result[0] = jnp.zeros((half, columns), jnp.float32)

        def send(block):
            return pltpu.make_async_copy(result.at[block], out_ref.at[block], done.at[block])

        for block in range(blocks):
            series = jnp.dot(table_ref[...], rebuilt[block], preferred_element_type=jnp.float32)
            result[block] += series[:half]
            result[block + 1] = series[half:]
            send(block).start()
        send(blocks).start()
        for block in range(blocks + 1):
            send(block).wait()

    return pl.pallas_call(
        kernel,
        out_shape=jax.ShapeDtypeStruct((blocks + 1, half, columns), jnp.float32),
        in_specs=[pl.BlockSpec(memory_space=pltpu.VMEM)] * 2,
        out_specs=pl.BlockSpec(memory_space=pl.ANY),
        scratch_shapes=[
            pltpu.VMEM((2, groups, blocks, lanes), jnp.float32),
            pltpu.VMEM((2, groups, blocks, lanes), jnp.float32),
            pltpu.VMEM((blocks, 2 * length, columns), jnp.bfloat16),
            pltpu.VMEM((blocks + 1, half, columns), jnp.float32),
            pltpu.SemaphoreType.DMA((blocks + 1,)),
        ],
        compiler_params=pltpu.CompilerParams(vmem_limit_bytes=32 * MIB),
        cost_estimate=pl.CostEstimate(
            flops=4 * length * length * blocks * columns,
            transcendentals=0,
            bytes_accessed=4 * (blocks + 1) * half * columns,
        ),
        name="synthesize",
    )(pieces, table)


def body(spectra, eigvecs, weights):
    _, freqs, blocks, points_dev = spectra.shape
    groups = lax.axis_size("freq")
    along_space = lax.axis_size("space")
    factor = 1.0 / math.sqrt(points_dev * along_space)
    partial = project(spectra, eigvecs, weights, along_space)
    terms = lax.all_to_all(partial, "space", split_axis=0, concat_axis=0, tiled=True)
    later_eigvecs, _ = lax.optimization_barrier((eigvecs, partial))
    pieces = add_coefficients(terms, cut_points(later_eigvecs, groups, blocks), factor)
    moved = lax.all_to_all(pieces, "freq", split_axis=0, concat_axis=0, tiled=True)
    filtered = synthesize(moved, transform_table(groups * freqs, groups), blocks)
    return filtered.reshape(-1, filtered.shape[-1])


def solution(mesh):
    placed = (P(None, "freq", None, "space"), P(None, "freq", None, "space"), P("space"))
    return jax.shard_map(
        body, mesh=mesh, in_specs=placed, out_specs=P(None, ("space", "freq")), check_vma=False
    )
```

```python
import math

import jax
import jax.numpy as jnp
import numpy as np
from jax import lax
from jax.experimental import pallas as pl
from jax.experimental.pallas import tpu as pltpu
from jax.sharding import PartitionSpec as P

MIB = 1024 * 1024
LANES = 128


def project(spectra, eigvecs, weights, parts):
    _, freqs, blocks, points = spectra.shape
    modes = eigvecs.shape[2]
    half = freqs * modes
    rows = 2 * freqs * blocks
    width = points // parts
    ends = [rows // 4, rows // 2, rows * 3 // 4, rows * 7 // 8, rows]
    starts = [0, *ends[:-1]]
    dtype = spectra.dtype

    def kernel(
        spectra_hbm, eigvecs_hbm, weights_hbm, out_ref, pieces_ref,
        spectra_ref, eigvecs_ref, weights_ref, weighted, columns, total, done,
    ):
        small = pltpu.make_async_copy(weights_hbm, weights_ref, done.at[0])
        small.start()
        by_part = [
            pltpu.make_async_copy(eigvecs_hbm.at[part], eigvecs_ref.at[part], done.at[1 + part])
            for part in range(2)
        ]
        for copy in by_part:
            copy.start()
        by_rows = []
        for i, (start, end) in enumerate(zip(starts, ends)):
            some = pl.ds(start, end - start)
            by_rows.append(
                pltpu.make_async_copy(spectra_hbm.at[some], spectra_ref.at[some], done.at[3 + i])
            )
            by_rows[-1].start()
        small.wait()
        per_row = weights_ref[...].astype(jnp.float32)
        scale = jnp.concatenate([per_row[i : i + 1] for i in range(points // LANES)], axis=1)
        for part in range(2):
            by_part[part].wait()
            for k in range(freqs):
                first = part * half + k * modes
                weighted[first : first + modes] = (
                    eigvecs_ref[part, k].astype(jnp.float32) * scale
                )
        columns[...] = jnp.transpose(weighted[...]).astype(dtype)
        for piece in range(parts):
            pieces_ref[piece] = eigvecs_ref[:, :, :, piece * width : (piece + 1) * width]
        for copy, start, end in zip(by_rows, starts, ends):
            copy.wait()
            total[start:end] = jnp.dot(
                spectra_ref[start:end], columns[...], preferred_element_type=jnp.float32
            )
        lane = lax.broadcasted_iota(jnp.int32, (blocks, 2 * half), 1)
        sums = []
        for part in range(2):
            kept = jnp.zeros((blocks, 2 * half), jnp.float32)
            for k in range(freqs):
                first = (part * freqs + k) * blocks
                own = (lane % half) // modes == k
                kept = jnp.where(own, total[first : first + blocks], kept)
            sums.append(kept)
        out_ref[...] = jnp.where(lane < half, sums[0], -sums[0]) + pltpu.roll(sums[1], half, 1)

    operands = (
        spectra.reshape(rows, points), eigvecs, weights.reshape(points // LANES, LANES)
    )
    return pl.pallas_call(
        kernel,
        out_shape=[
            jax.ShapeDtypeStruct((blocks, 2 * half), jnp.float32),
            jax.ShapeDtypeStruct((parts, 2, freqs, modes, width), dtype),
        ],
        in_specs=[pl.BlockSpec(memory_space=pl.ANY)] * 3,
        out_specs=[pl.BlockSpec(memory_space=pltpu.VMEM)] * 2,
        scratch_shapes=[
            pltpu.VMEM((rows, points), dtype),
            pltpu.VMEM(eigvecs.shape, dtype),
            pltpu.VMEM((points // LANES, LANES), dtype),
            pltpu.VMEM((2 * half, points), jnp.float32),
            pltpu.VMEM((points, 2 * half), dtype),
            pltpu.VMEM((rows, 2 * half), jnp.float32),
            pltpu.SemaphoreType.DMA((3 + len(ends),)),
        ],
        compiler_params=pltpu.CompilerParams(vmem_limit_bytes=32 * MIB),
        cost_estimate=pl.CostEstimate(
            flops=8 * freqs * blocks * modes * points,
            transcendentals=0,
            bytes_accessed=2 * (spectra.size + eigvecs.size),
        ),
        name="project",
    )(*(pltpu.with_memory_space_constraint(operand, pltpu.HBM) for operand in operands))


def gather_terms(chip, arrived, beside, factor, copies):
    def kernel(chip_ref, arrived_ref, beside_ref, out_ref):
        value = (chip_ref[...] + arrived_ref[...] + beside_ref[...]) * factor
        for copy in range(copies):
            out_ref[copy] = value

    return pl.pallas_call(
        kernel,
        out_shape=jax.ShapeDtypeStruct((copies, *chip.shape), chip.dtype),
        in_specs=[pl.BlockSpec(memory_space=pltpu.VMEM)] * 3,
        out_specs=pl.BlockSpec(memory_space=pltpu.VMEM),
        compiler_params=pltpu.CompilerParams(vmem_limit_bytes=4 * MIB),
        cost_estimate=pl.CostEstimate(
            flops=3 * chip.size, transcendentals=0, bytes_accessed=4 * copies * chip.size
        ),
        name="gather_terms",
    )(chip, arrived, beside)


def sum_over_space(partial, factor, copies):
    count = lax.axis_size("space")
    chips = count // 2

    def beside(value):
        return lax.ppermute(value, "space", [(i, i ^ 1) for i in range(count)])

    def around(value, hops):
        pairs = [(2 * z, 2 * ((z + hops) % chips)) for z in range(chips)]
        if 2 * hops != chips:
            pairs += [(2 * z + 1, 2 * ((z - hops) % chips) + 1) for z in range(chips)]
        return lax.ppermute(value, "space", pairs)

    chip = partial + beside(partial)
    arrived = sum(around(chip, hops) for hops in range(1, chips // 2 + 1))
    return gather_terms(chip, arrived, beside(arrived), factor, copies)


def transform_table(length, groups):
    sample = np.arange(length)
    phase = 2.0 * np.pi * ((sample[:, None] * sample[None, :]) % length) / length
    window = np.sin(np.pi * (sample + 0.5) / length) / math.sqrt(length)
    table = np.stack([np.cos(phase), -np.sin(phase)], axis=1) * window[:, None, None]
    table = table.reshape(length, 2, groups, length // groups).transpose(0, 2, 1, 3)
    return jnp.asarray(table.reshape(length, 2 * length), jnp.bfloat16)


def synthesize(coefficients, moved_modes, table):
    groups, blocks, lanes = coefficients.shape
    columns = moved_modes.shape[2]
    length = table.shape[0]
    freqs = length // groups
    modes = lanes // (2 * freqs)
    half_lanes = lanes // 2
    half = length // 2

    def kernel(coef_ref, modes_ref, table_ref, out_ref, high, low, rebuilt, result, done):
        lane = lax.broadcasted_iota(jnp.int32, (freqs, lanes), 1)
        row = lax.broadcasted_iota(jnp.int32, (freqs, lanes), 0)
        own = jnp.where((lane % half_lanes) // modes == row, 1.0, 0.0)
        signed = jnp.where(lane < half_lanes, own, -own)
        for group in range(groups):
            plain = coef_ref[group]
            for kind, value in enumerate((plain, pltpu.roll(plain, half_lanes, 1))):
                rounded = value.astype(jnp.bfloat16).astype(jnp.float32)
                high[kind, group] = rounded
                low[kind, group] = value - rounded
        for group in range(groups):
            tiles = []
            for block in range(blocks):
                for kind, mask in enumerate((signed, own)):
                    tiles.append(
                        jnp.concatenate(
                            [
                                (jnp.broadcast_to(
                                    side[kind, group, pl.ds(block, 1), :], (freqs, lanes)
                                ) * mask).astype(jnp.bfloat16)
                                for side in (high, low)
                            ],
                            axis=1,
                        )
                    )
            values = modes_ref[group]
            product = jnp.dot(
                jnp.concatenate(tiles, axis=0),
                jnp.concatenate([values, values], axis=0),
                preferred_element_type=jnp.float32,
            )
            rebuilt[:, group * 2 * freqs : (group + 1) * 2 * freqs, :] = product.astype(
                jnp.bfloat16
            ).reshape(blocks, 2 * freqs, columns)
        result[0] = jnp.zeros((half, columns), jnp.float32)

        def send(block):
            return pltpu.make_async_copy(result.at[block], out_ref.at[block], done.at[block])

        for block in range(blocks):
            series = jnp.dot(table_ref[...], rebuilt[block], preferred_element_type=jnp.float32)
            result[block] += series[:half]
            result[block + 1] = series[half:]
            send(block).start()
        send(blocks).start()
        for block in range(blocks + 1):
            send(block).wait()

    return pl.pallas_call(
        kernel,
        out_shape=jax.ShapeDtypeStruct((blocks + 1, half, columns), jnp.float32),
        in_specs=[pl.BlockSpec(memory_space=pltpu.VMEM)] * 3,
        out_specs=pl.BlockSpec(memory_space=pl.ANY),
        scratch_shapes=[
            pltpu.VMEM((2, groups, blocks, lanes), jnp.float32),
            pltpu.VMEM((2, groups, blocks, lanes), jnp.float32),
            pltpu.VMEM((blocks, 2 * length, columns), jnp.bfloat16),
            pltpu.VMEM((blocks + 1, half, columns), jnp.float32),
            pltpu.SemaphoreType.DMA((blocks + 1,)),
        ],
        compiler_params=pltpu.CompilerParams(vmem_limit_bytes=32 * MIB),
        cost_estimate=pl.CostEstimate(
            flops=4 * length * length * blocks * columns,
            transcendentals=0,
            bytes_accessed=4 * (blocks + 1) * half * columns,
        ),
        name="synthesize",
    )(coefficients, moved_modes, table)


def body(spectra, eigvecs, weights):
    _, freqs, _, points_dev = spectra.shape
    groups = lax.axis_size("freq")
    factor = 1.0 / math.sqrt(points_dev * lax.axis_size("space"))
    partial, pieces = project(spectra, eigvecs, weights, groups)
    moved = lax.all_to_all(pieces, "freq", split_axis=0, concat_axis=0, tiled=True)
    copies = sum_over_space(partial, factor, groups)
    copies, moved = lax.optimization_barrier((copies, moved))
    gathered = lax.all_to_all(copies, "freq", split_axis=0, concat_axis=0, tiled=True)
    filtered = synthesize(
        gathered,
        moved.reshape(groups, -1, moved.shape[-1]),
        transform_table(groups * freqs, groups),
    )
    return filtered.reshape(-1, filtered.shape[-1])


def solution(mesh):
    placed = (P(None, "freq", None, "space"), P(None, "freq", None, "space"), P("space"))
    return jax.shard_map(
        body, mesh=mesh, in_specs=placed, out_specs=P(None, ("space", "freq")), check_vma=False
    )
```

```python
import math

import jax
import jax.numpy as jnp
import numpy as np
from jax import lax
from jax.experimental import pallas as pl
from jax.experimental.pallas import tpu as pltpu
from jax.sharding import PartitionSpec as P

MIB = 1024 * 1024
LANES = 128
SLAB = 4
HOPS_BY_CORE = ((0, -2), (-1, 2), (1, 3), (4, -3))


def project(spectra, eigvecs, weights, parts):
    _, freqs, blocks, points = spectra.shape
    modes = eigvecs.shape[2]
    half = freqs * modes
    rows = 2 * freqs * blocks
    width = points // parts
    ends = [rows // 4, rows // 2, rows * 3 // 4, rows * 7 // 8, rows]
    starts = [0, *ends[:-1]]
    dtype = spectra.dtype

    def kernel(
        spectra_hbm, eigvecs_hbm, weights_hbm, out_ref, pieces_hbm,
        spectra_ref, eigvecs_ref, weights_ref, weighted, columns, total, pieces_ref, done, sent,
    ):
        small = pltpu.make_async_copy(weights_hbm, weights_ref, done.at[0])
        small.start()
        by_part = [
            pltpu.make_async_copy(eigvecs_hbm.at[part], eigvecs_ref.at[part], done.at[1 + part])
            for part in range(2)
        ]
        for copy in by_part:
            copy.start()
        by_rows = []
        for i, (start, end) in enumerate(zip(starts, ends)):
            some = pl.ds(start, end - start)
            by_rows.append(
                pltpu.make_async_copy(spectra_hbm.at[some], spectra_ref.at[some], done.at[3 + i])
            )
            by_rows[-1].start()
        small.wait()
        per_row = weights_ref[...].astype(jnp.float32)
        scale = jnp.concatenate([per_row[i : i + 1] for i in range(points // LANES)], axis=1)
        for part in range(2):
            by_part[part].wait()
            for k in range(freqs):
                first = part * half + k * modes
                weighted[first : first + modes] = (
                    eigvecs_ref[part, k].astype(jnp.float32) * scale
                )
        columns[...] = jnp.transpose(weighted[...]).astype(dtype)
        slabs = []
        for piece in range(parts):
            pieces_ref[piece] = eigvecs_ref[:, :, :, piece * width : (piece + 1) * width]
            if piece % SLAB == SLAB - 1:
                some = pl.ds(piece + 1 - SLAB, SLAB)
                slabs.append(
                    pltpu.make_async_copy(
                        pieces_ref.at[some], pieces_hbm.at[some], sent.at[len(slabs)]
                    )
                )
                slabs[-1].start()
        for copy, start, end in zip(by_rows, starts, ends):
            copy.wait()
            total[start:end] = jnp.dot(
                spectra_ref[start:end], columns[...], preferred_element_type=jnp.float32
            )
        lane = lax.broadcasted_iota(jnp.int32, (blocks, 2 * half), 1)
        sums = []
        for part in range(2):
            kept = jnp.zeros((blocks, 2 * half), jnp.float32)
            for k in range(freqs):
                first = (part * freqs + k) * blocks
                own = (lane % half) // modes == k
                kept = jnp.where(own, total[first : first + blocks], kept)
            sums.append(kept)
        out_ref[...] = jnp.where(lane < half, sums[0], -sums[0]) + pltpu.roll(sums[1], half, 1)
        for copy in slabs:
            copy.wait()

    operands = (
        spectra.reshape(rows, points), eigvecs, weights.reshape(points // LANES, LANES)
    )
    return pl.pallas_call(
        kernel,
        out_shape=[
            jax.ShapeDtypeStruct((blocks, 2 * half), jnp.float32),
            jax.ShapeDtypeStruct((parts, 2, freqs, modes, width), dtype),
        ],
        in_specs=[pl.BlockSpec(memory_space=pl.ANY)] * 3,
        out_specs=[pl.BlockSpec(memory_space=pltpu.VMEM), pl.BlockSpec(memory_space=pl.ANY)],
        scratch_shapes=[
            pltpu.VMEM((rows, points), dtype),
            pltpu.VMEM(eigvecs.shape, dtype),
            pltpu.VMEM((points // LANES, LANES), dtype),
            pltpu.VMEM((2 * half, points), jnp.float32),
            pltpu.VMEM((points, 2 * half), dtype),
            pltpu.VMEM((rows, 2 * half), jnp.float32),
            pltpu.VMEM((parts, 2, freqs, modes, width), dtype),
            pltpu.SemaphoreType.DMA((3 + len(ends),)),
            pltpu.SemaphoreType.DMA((parts // SLAB,)),
        ],
        compiler_params=pltpu.CompilerParams(vmem_limit_bytes=32 * MIB),
        cost_estimate=pl.CostEstimate(
            flops=8 * freqs * blocks * modes * points,
            transcendentals=0,
            bytes_accessed=2 * (spectra.size + eigvecs.size),
        ),
        name="project",
    )(*(pltpu.with_memory_space_constraint(operand, pltpu.HBM) for operand in operands))


def gather_terms(chip, arrived, beside, factor, copies):
    def kernel(chip_ref, arrived_ref, beside_ref, out_ref):
        value = (chip_ref[...] + arrived_ref[...] + beside_ref[...]) * factor
        for copy in range(copies):
            out_ref[copy] = value

    return pl.pallas_call(
        kernel,
        out_shape=pltpu.VMEM((copies, *chip.shape), chip.dtype),
        in_specs=[pl.BlockSpec(memory_space=pltpu.VMEM)] * 3,
        out_specs=pl.BlockSpec(memory_space=pltpu.VMEM),
        compiler_params=pltpu.CompilerParams(vmem_limit_bytes=4 * MIB),
        cost_estimate=pl.CostEstimate(
            flops=3 * chip.size, transcendentals=0, bytes_accessed=4 * copies * chip.size
        ),
        name="gather_terms",
    )(chip, arrived, beside)


def sum_over_space(partial, factor, copies):
    count = lax.axis_size("space")
    chips = count // 2

    def beside(value):
        return lax.ppermute(value, "space", [(i, i ^ 1) for i in range(count)])

    def around(value, by_core):
        pairs = []
        for core, hops in enumerate(by_core):
            if hops:
                pairs += [
                    (2 * z + core, 2 * ((z + hops) % chips) + core) for z in range(chips)
                ]
        return lax.ppermute(value, "space", pairs)

    chip = partial + beside(partial)
    arrived = sum(around(chip, by_core) for by_core in HOPS_BY_CORE)
    return gather_terms(chip, arrived, beside(arrived), factor, copies)


def transform_table(length, groups):
    sample = np.arange(length)
    phase = 2.0 * np.pi * ((sample[:, None] * sample[None, :]) % length) / length
    window = np.sin(np.pi * (sample + 0.5) / length) / math.sqrt(length)
    table = np.stack([np.cos(phase), -np.sin(phase)], axis=1) * window[:, None, None]
    table = table.reshape(length, 2, groups, length // groups).transpose(0, 2, 1, 3)
    return jnp.asarray(table.reshape(length, 2 * length), jnp.bfloat16)


def synthesize(coefficients, moved_modes, table):
    groups, blocks, lanes = coefficients.shape
    columns = moved_modes.shape[2]
    length = table.shape[0]
    freqs = length // groups
    modes = lanes // (2 * freqs)
    half_lanes = lanes // 2
    half = length // 2

    def kernel(coef_ref, modes_ref, table_ref, out_ref, high, low, rebuilt, result, done):
        lane = lax.broadcasted_iota(jnp.int32, (freqs, lanes), 1)
        row = lax.broadcasted_iota(jnp.int32, (freqs, lanes), 0)
        own = jnp.where((lane % half_lanes) // modes == row, 1.0, 0.0)
        signed = jnp.where(lane < half_lanes, own, -own)
        for group in range(groups):
            plain = coef_ref[group]
            for kind, value in enumerate((plain, pltpu.roll(plain, half_lanes, 1))):
                rounded = value.astype(jnp.bfloat16).astype(jnp.float32)
                high[kind, group] = rounded
                low[kind, group] = value - rounded
        for group in range(groups):
            tiles = []
            for block in range(blocks):
                for kind, mask in enumerate((signed, own)):
                    tiles.append(
                        jnp.concatenate(
                            [
                                (jnp.broadcast_to(
                                    side[kind, group, pl.ds(block, 1), :], (freqs, lanes)
                                ) * mask).astype(jnp.bfloat16)
                                for side in (high, low)
                            ],
                            axis=1,
                        )
                    )
            values = modes_ref[group]
            product = jnp.dot(
                jnp.concatenate(tiles, axis=0),
                jnp.concatenate([values, values], axis=0),
                preferred_element_type=jnp.float32,
            )
            rebuilt[:, group * 2 * freqs : (group + 1) * 2 * freqs, :] = product.astype(
                jnp.bfloat16
            ).reshape(blocks, 2 * freqs, columns)
        result[0] = jnp.zeros((half, columns), jnp.float32)

        def send(block):
            return pltpu.make_async_copy(result.at[block], out_ref.at[block], done.at[block])

        for block in range(blocks):
            series = jnp.dot(table_ref[...], rebuilt[block], preferred_element_type=jnp.float32)
            result[block] += series[:half]
            result[block + 1] = series[half:]
            send(block).start()
        send(blocks).start()
        for block in range(blocks + 1):
            send(block).wait()

    return pl.pallas_call(
        kernel,
        out_shape=jax.ShapeDtypeStruct((blocks + 1, half, columns), jnp.float32),
        in_specs=[pl.BlockSpec(memory_space=pltpu.VMEM)] * 3,
        out_specs=pl.BlockSpec(memory_space=pl.ANY),
        scratch_shapes=[
            pltpu.VMEM((2, groups, blocks, lanes), jnp.float32),
            pltpu.VMEM((2, groups, blocks, lanes), jnp.float32),
            pltpu.VMEM((blocks, 2 * length, columns), jnp.bfloat16),
            pltpu.VMEM((blocks + 1, half, columns), jnp.float32),
            pltpu.SemaphoreType.DMA((blocks + 1,)),
        ],
        compiler_params=pltpu.CompilerParams(vmem_limit_bytes=32 * MIB),
        cost_estimate=pl.CostEstimate(
            flops=4 * length * length * blocks * columns,
            transcendentals=0,
            bytes_accessed=4 * (blocks + 1) * half * columns,
        ),
        name="synthesize",
    )(coefficients, moved_modes, table)


def body(spectra, eigvecs, weights):
    _, freqs, _, points_dev = spectra.shape
    groups = lax.axis_size("freq")
    factor = 1.0 / math.sqrt(points_dev * lax.axis_size("space"))
    partial, pieces = project(spectra, eigvecs, weights, groups)
    moved = lax.all_to_all(pieces, "freq", split_axis=0, concat_axis=0, tiled=True)
    copies = sum_over_space(partial, factor, groups)
    copies, moved = lax.optimization_barrier((copies, moved))
    gathered = lax.all_to_all(copies, "freq", split_axis=0, concat_axis=0, tiled=True)
    filtered = synthesize(
        gathered,
        moved.reshape(groups, -1, moved.shape[-1]),
        transform_table(groups * freqs, groups),
    )
    return filtered.reshape(-1, filtered.shape[-1])


def solution(mesh):
    placed = (P(None, "freq", None, "space"), P(None, "freq", None, "space"), P("space"))
    return jax.shard_map(
        body, mesh=mesh, in_specs=placed, out_specs=P(None, ("space", "freq")), check_vma=False
    )
```

```python
import math

import jax
import jax.numpy as jnp
import numpy as np
from jax import lax
from jax.experimental import pallas as pl
from jax.experimental.pallas import tpu as pltpu
from jax.sharding import PartitionSpec as P

MIB = 1024 * 1024
LANES = 128
SLAB = 4
HOPS_BY_CORE = ((0, -2), (-1, 2), (1, 3), (4, -3))


def project(spectra, eigvecs, weights, parts):
    _, freqs, blocks, points = spectra.shape
    modes = eigvecs.shape[2]
    half = freqs * modes
    rows = 2 * freqs * blocks
    width = points // parts
    ends = [rows * (i + 1) // 4 for i in range(4)]
    starts = [0, *ends[:-1]]
    dtype = spectra.dtype

    def kernel(
        spectra_hbm, eigvecs_hbm, weights_hbm, out_ref, pieces_hbm,
        spectra_ref, eigvecs_ref, weights_ref, weighted, columns, total, pieces_ref, done, sent,
    ):
        small = pltpu.make_async_copy(weights_hbm, weights_ref, done.at[0])
        small.start()
        by_part = [
            pltpu.make_async_copy(eigvecs_hbm.at[part], eigvecs_ref.at[part], done.at[1 + part])
            for part in range(2)
        ]
        for copy in by_part:
            copy.start()
        by_rows = []
        for i, (start, end) in enumerate(zip(starts, ends)):
            some = pl.ds(start, end - start)
            by_rows.append(
                pltpu.make_async_copy(spectra_hbm.at[some], spectra_ref.at[some], done.at[3 + i])
            )
            by_rows[-1].start()
        small.wait()
        per_row = weights_ref[...].astype(jnp.float32)
        scale = jnp.concatenate([per_row[i : i + 1] for i in range(points // LANES)], axis=1)
        for part in range(2):
            by_part[part].wait()
            for k in range(freqs):
                first = part * half + k * modes
                weighted[first : first + modes] = (
                    eigvecs_ref[part, k].astype(jnp.float32) * scale
                )
        columns[...] = jnp.transpose(weighted[...]).astype(dtype)
        slabs = []
        for piece in range(parts):
            pieces_ref[piece] = eigvecs_ref[:, :, :, piece * width : (piece + 1) * width]
            if piece % SLAB == SLAB - 1:
                some = pl.ds(piece + 1 - SLAB, SLAB)
                slabs.append(
                    pltpu.make_async_copy(
                        pieces_ref.at[some], pieces_hbm.at[some], sent.at[len(slabs)]
                    )
                )
                slabs[-1].start()
        for copy, start, end in zip(by_rows, starts, ends):
            copy.wait()
            total[start:end] = jnp.dot(
                spectra_ref[start:end], columns[...], preferred_element_type=jnp.float32
            )
        lane = lax.broadcasted_iota(jnp.int32, (blocks, 2 * half), 1)
        sums = []
        for part in range(2):
            kept = jnp.zeros((blocks, 2 * half), jnp.float32)
            for k in range(freqs):
                first = (part * freqs + k) * blocks
                own = (lane % half) // modes == k
                kept = jnp.where(own, total[first : first + blocks], kept)
            sums.append(kept)
        out_ref[...] = jnp.where(lane < half, sums[0], -sums[0]) + pltpu.roll(sums[1], half, 1)
        for copy in slabs:
            copy.wait()

    operands = (
        spectra.reshape(rows, points), eigvecs, weights.reshape(points // LANES, LANES)
    )
    return pl.pallas_call(
        kernel,
        out_shape=[
            jax.ShapeDtypeStruct((blocks, 2 * half), jnp.float32),
            jax.ShapeDtypeStruct((parts, 2, freqs, modes, width), dtype),
        ],
        in_specs=[pl.BlockSpec(memory_space=pl.ANY)] * 3,
        out_specs=[pl.BlockSpec(memory_space=pltpu.VMEM), pl.BlockSpec(memory_space=pl.ANY)],
        scratch_shapes=[
            pltpu.VMEM((rows, points), dtype),
            pltpu.VMEM(eigvecs.shape, dtype),
            pltpu.VMEM((points // LANES, LANES), dtype),
            pltpu.VMEM((2 * half, points), jnp.float32),
            pltpu.VMEM((points, 2 * half), dtype),
            pltpu.VMEM((rows, 2 * half), jnp.float32),
            pltpu.VMEM((parts, 2, freqs, modes, width), dtype),
            pltpu.SemaphoreType.DMA((3 + len(ends),)),
            pltpu.SemaphoreType.DMA((parts // SLAB,)),
        ],
        compiler_params=pltpu.CompilerParams(vmem_limit_bytes=32 * MIB),
        cost_estimate=pl.CostEstimate(
            flops=8 * freqs * blocks * modes * points,
            transcendentals=0,
            bytes_accessed=2 * (spectra.size + eigvecs.size),
        ),
        name="project",
    )(*(pltpu.with_memory_space_constraint(operand, pltpu.HBM) for operand in operands))


def gather_terms(chip, arrived, beside, factor, copies):
    def kernel(chip_ref, arrived_ref, beside_ref, out_ref):
        value = (chip_ref[...] + arrived_ref[...] + beside_ref[...]) * factor
        for copy in range(copies):
            out_ref[copy] = value

    return pl.pallas_call(
        kernel,
        out_shape=pltpu.VMEM((copies, *chip.shape), chip.dtype),
        in_specs=[pl.BlockSpec(memory_space=pltpu.VMEM)] * 3,
        out_specs=pl.BlockSpec(memory_space=pltpu.VMEM),
        compiler_params=pltpu.CompilerParams(vmem_limit_bytes=4 * MIB),
        cost_estimate=pl.CostEstimate(
            flops=3 * chip.size, transcendentals=0, bytes_accessed=4 * copies * chip.size
        ),
        name="gather_terms",
    )(chip, arrived, beside)


def sum_over_space(partial, factor, copies):
    count = lax.axis_size("space")
    chips = count // 2

    def beside(value):
        return lax.ppermute(value, "space", [(i, i ^ 1) for i in range(count)])

    def around(value, by_core):
        pairs = []
        for core, hops in enumerate(by_core):
            if hops:
                pairs += [
                    (2 * z + core, 2 * ((z + hops) % chips) + core) for z in range(chips)
                ]
        return lax.ppermute(value, "space", pairs)

    chip = partial + beside(partial)
    arrived = sum(around(chip, by_core) for by_core in HOPS_BY_CORE)
    return gather_terms(chip, arrived, beside(arrived), factor, copies)


def transform_tables(length, groups):
    freqs = length // groups
    sample = np.arange(length // 2)
    phase = 2.0 * np.pi * ((sample[:, None] * np.arange(length)[None, :]) % length) / length
    table = np.stack([np.cos(phase), -np.sin(phase)], axis=1) / math.sqrt(length)
    table = table.reshape(length // 2, 2, groups, freqs // 2, 2).transpose(4, 0, 2, 1, 3)
    window = np.sin(np.pi * (np.arange(length) + 0.5) / length).reshape(2, length // 2, 1)
    return (
        jnp.asarray(table.reshape(2, length // 2, length), jnp.bfloat16),
        jnp.asarray(np.broadcast_to(window, (2, length // 2, LANES)), jnp.float32),
    )


def synthesize(coefficients, moved_modes, table, window):
    groups, blocks, lanes = coefficients.shape
    columns = moved_modes.shape[2]
    length = table.shape[2]
    freqs = length // groups
    modes = lanes // (2 * freqs)
    half_lanes = lanes // 2
    half = length // 2
    pair = freqs // 2

    def kernel(
        coef_ref, modes_ref, table_ref, window_ref, out_ref, high, low, rebuilt, result, done
    ):
        lane = lax.broadcasted_iota(jnp.int32, (freqs, lanes), 1)
        row = lax.broadcasted_iota(jnp.int32, (freqs, lanes), 0)
        sign = jnp.where((row < pair) & (lane >= half_lanes), -1.0, 1.0)
        masks = [
            jnp.where((lane % half_lanes) // modes == 2 * (row % pair) + odd, sign, 0.0)
            for odd in range(2)
        ]
        for group in range(groups):
            plain = coef_ref[group]
            for kind, value in enumerate((plain, pltpu.roll(plain, half_lanes, 1))):
                rounded = value.astype(jnp.bfloat16).astype(jnp.float32)
                high[kind, group] = rounded
                low[kind, group] = value - rounded
        first = jnp.concatenate([window_ref[0]] * (columns // LANES), axis=1)
        second = jnp.concatenate([window_ref[1]] * (columns // LANES), axis=1)
        result[0] = jnp.zeros((half, columns), jnp.float32)

        def send(block):
            return pltpu.make_async_copy(result.at[block], out_ref.at[block], done.at[block])

        for group in range(groups):
            tiles = []
            for block in range(blocks):
                rows = [
                    jnp.concatenate(
                        [
                            jnp.broadcast_to(
                                side[kind, group, pl.ds(block, 1), :], (pair, lanes)
                            )
                            for kind in range(2)
                        ],
                        axis=0,
                    )
                    for side in (high, low)
                ]
                for mask in masks:
                    tiles.append(
                        jnp.concatenate(
                            [(both * mask).astype(jnp.bfloat16) for both in rows], axis=1
                        )
                    )
            values = modes_ref[group]
            product = jnp.dot(
                jnp.concatenate(tiles, axis=0),
                jnp.concatenate([values, values], axis=0),
                preferred_element_type=jnp.float32,
            )
            rebuilt[:, :, group * freqs : (group + 1) * freqs, :] = product.astype(
                jnp.bfloat16
            ).reshape(blocks, 2, freqs, columns)
        for block in range(blocks):
            even, odd = (
                jnp.dot(table_ref[i], rebuilt[block, i], preferred_element_type=jnp.float32)
                for i in range(2)
            )
            result[block] += (even + odd) * first
            result[block + 1] = (even - odd) * second
            send(block).start()
        send(blocks).start()
        for block in range(blocks + 1):
            send(block).wait()

    return pl.pallas_call(
        kernel,
        out_shape=jax.ShapeDtypeStruct((blocks + 1, half, columns), jnp.float32),
        in_specs=[pl.BlockSpec(memory_space=pltpu.VMEM)] * 4,
        out_specs=pl.BlockSpec(memory_space=pl.ANY),
        scratch_shapes=[
            pltpu.VMEM((2, groups, blocks, lanes), jnp.float32),
            pltpu.VMEM((2, groups, blocks, lanes), jnp.float32),
            pltpu.VMEM((blocks, 2, length, columns), jnp.bfloat16),
            pltpu.VMEM((blocks + 1, half, columns), jnp.float32),
            pltpu.SemaphoreType.DMA((blocks + 1,)),
        ],
        compiler_params=pltpu.CompilerParams(vmem_limit_bytes=32 * MIB),
        cost_estimate=pl.CostEstimate(
            flops=2 * length * length * blocks * columns,
            transcendentals=0,
            bytes_accessed=4 * (blocks + 1) * half * columns,
        ),
        name="synthesize",
    )(coefficients, moved_modes, table, window)


def body(spectra, eigvecs, weights):
    _, freqs, _, points_dev = spectra.shape
    groups = lax.axis_size("freq")
    factor = 1.0 / math.sqrt(points_dev * lax.axis_size("space"))
    partial, pieces = project(spectra, eigvecs, weights, groups)
    moved = lax.all_to_all(pieces, "freq", split_axis=0, concat_axis=0, tiled=True)
    copies = sum_over_space(partial, factor, groups)
    copies, moved = lax.optimization_barrier((copies, moved))
    gathered = lax.all_to_all(copies, "freq", split_axis=0, concat_axis=0, tiled=True)
    filtered = synthesize(
        gathered,
        moved.reshape(groups, -1, moved.shape[-1]),
        *transform_tables(groups * freqs, groups),
    )
    return filtered.reshape(-1, filtered.shape[-1])


def solution(mesh):
    placed = (P(None, "freq", None, "space"), P(None, "freq", None, "space"), P("space"))
    return jax.shard_map(
        body, mesh=mesh, in_specs=placed, out_specs=P(None, ("space", "freq")), check_vma=False
    )
```

```python
import math

import jax
import jax.numpy as jnp
import numpy as np
from jax import lax
from jax.experimental import pallas as pl
from jax.experimental.pallas import tpu as pltpu
from jax.sharding import PartitionSpec as P

MIB = 1024 * 1024
LANES = 128
SLAB = 4
HOPS_BY_CORE = ((0, 1), (-1, 2), (-2, -3), (4, 3))


def project(spectra, eigvecs, weights, parts):
    _, freqs, blocks, points = spectra.shape
    modes = eigvecs.shape[2]
    half = freqs * modes
    rows = 2 * freqs * blocks
    width = points // parts
    ends = [rows * (i + 1) // 4 for i in range(4)]
    starts = [0, *ends[:-1]]
    dtype = spectra.dtype

    def kernel(
        spectra_hbm, eigvecs_hbm, weights_hbm, out_ref, pieces_hbm,
        spectra_ref, eigvecs_ref, weights_ref, weighted, columns, total, pieces_ref, done, sent,
    ):
        small = pltpu.make_async_copy(weights_hbm, weights_ref, done.at[0])
        small.start()
        by_part = [
            pltpu.make_async_copy(eigvecs_hbm.at[part], eigvecs_ref.at[part], done.at[1 + part])
            for part in range(2)
        ]
        for copy in by_part:
            copy.start()
        by_rows = []
        for i, (start, end) in enumerate(zip(starts, ends)):
            some = pl.ds(start, end - start)
            by_rows.append(
                pltpu.make_async_copy(spectra_hbm.at[some], spectra_ref.at[some], done.at[3 + i])
            )
            by_rows[-1].start()
        small.wait()
        per_row = weights_ref[...].astype(jnp.float32)
        scale = jnp.concatenate([per_row[i : i + 1] for i in range(points // LANES)], axis=1)
        for part in range(2):
            by_part[part].wait()
            for k in range(freqs):
                first = part * half + k * modes
                weighted[first : first + modes] = (
                    eigvecs_ref[part, k].astype(jnp.float32) * scale
                )
        columns[...] = jnp.transpose(weighted[...]).astype(dtype)
        slabs = []
        for piece in range(parts):
            pieces_ref[piece] = eigvecs_ref[:, :, :, piece * width : (piece + 1) * width]
            if piece % SLAB == SLAB - 1:
                some = pl.ds(piece + 1 - SLAB, SLAB)
                slabs.append(
                    pltpu.make_async_copy(
                        pieces_ref.at[some], pieces_hbm.at[some], sent.at[len(slabs)]
                    )
                )
                slabs[-1].start()
        for copy, start, end in zip(by_rows, starts, ends):
            copy.wait()
            total[start:end] = jnp.dot(
                spectra_ref[start:end], columns[...], preferred_element_type=jnp.float32
            )
        lane = lax.broadcasted_iota(jnp.int32, (blocks, 2 * half), 1)
        sums = []
        for part in range(2):
            kept = jnp.zeros((blocks, 2 * half), jnp.float32)
            for k in range(freqs):
                first = (part * freqs + k) * blocks
                own = (lane % half) // modes == k
                kept = jnp.where(own, total[first : first + blocks], kept)
            sums.append(kept)
        out_ref[...] = jnp.where(lane < half, sums[0], -sums[0]) + pltpu.roll(sums[1], half, 1)
        for copy in slabs:
            copy.wait()

    operands = (
        spectra.reshape(rows, points), eigvecs, weights.reshape(points // LANES, LANES)
    )
    return pl.pallas_call(
        kernel,
        out_shape=[
            jax.ShapeDtypeStruct((blocks, 2 * half), jnp.float32),
            jax.ShapeDtypeStruct((parts, 2, freqs, modes, width), dtype),
        ],
        in_specs=[pl.BlockSpec(memory_space=pl.ANY)] * 3,
        out_specs=[pl.BlockSpec(memory_space=pltpu.VMEM), pl.BlockSpec(memory_space=pl.ANY)],
        scratch_shapes=[
            pltpu.VMEM((rows, points), dtype),
            pltpu.VMEM(eigvecs.shape, dtype),
            pltpu.VMEM((points // LANES, LANES), dtype),
            pltpu.VMEM((2 * half, points), jnp.float32),
            pltpu.VMEM((points, 2 * half), dtype),
            pltpu.VMEM((rows, 2 * half), jnp.float32),
            pltpu.VMEM((parts, 2, freqs, modes, width), dtype),
            pltpu.SemaphoreType.DMA((3 + len(ends),)),
            pltpu.SemaphoreType.DMA((parts // SLAB,)),
        ],
        compiler_params=pltpu.CompilerParams(vmem_limit_bytes=32 * MIB),
        cost_estimate=pl.CostEstimate(
            flops=8 * freqs * blocks * modes * points,
            transcendentals=0,
            bytes_accessed=2 * (spectra.size + eigvecs.size),
        ),
        name="project",
    )(*(pltpu.with_memory_space_constraint(operand, pltpu.HBM) for operand in operands))


def gather_terms(chip, arrived, beside, factor, copies):
    def kernel(chip_ref, arrived_ref, beside_ref, out_ref):
        value = (chip_ref[...] + arrived_ref[...] + beside_ref[...]) * factor
        for copy in range(copies):
            out_ref[copy] = value

    return pl.pallas_call(
        kernel,
        out_shape=pltpu.VMEM((copies, *chip.shape), chip.dtype),
        in_specs=[pl.BlockSpec(memory_space=pltpu.VMEM)] * 3,
        out_specs=pl.BlockSpec(memory_space=pltpu.VMEM),
        compiler_params=pltpu.CompilerParams(vmem_limit_bytes=4 * MIB),
        cost_estimate=pl.CostEstimate(
            flops=3 * chip.size, transcendentals=0, bytes_accessed=4 * copies * chip.size
        ),
        name="gather_terms",
    )(chip, arrived, beside)


def sum_over_space(partial, factor, copies):
    count = lax.axis_size("space")
    chips = count // 2

    def beside(value):
        return lax.ppermute(value, "space", [(i, i ^ 1) for i in range(count)])

    def around(value, by_core):
        pairs = []
        for core, hops in enumerate(by_core):
            if hops:
                pairs += [
                    (2 * z + core, 2 * ((z + hops) % chips) + core) for z in range(chips)
                ]
        return lax.ppermute(value, "space", pairs)

    chip = partial + beside(partial)
    arrived = sum(around(chip, by_core) for by_core in HOPS_BY_CORE)
    return gather_terms(chip, arrived, beside(arrived), factor, copies)


def transform_tables(length, groups):
    freqs = length // groups
    sample = np.arange(length // 2)
    phase = 2.0 * np.pi * ((sample[:, None] * np.arange(length)[None, :]) % length) / length
    table = np.stack([np.cos(phase), -np.sin(phase)], axis=1) / math.sqrt(length)
    table = table.reshape(length // 2, 2, groups, freqs // 2, 2).transpose(4, 0, 2, 1, 3)
    window = np.sin(np.pi * (np.arange(length) + 0.5) / length).reshape(2, length // 2, 1)
    return (
        jnp.asarray(table.reshape(2, length // 2, length), jnp.bfloat16),
        jnp.asarray(np.broadcast_to(window, (2, length // 2, LANES)), jnp.float32),
    )


def synthesize(coefficients, moved_modes, table, window):
    groups, blocks, lanes = coefficients.shape
    columns = moved_modes.shape[2]
    length = table.shape[2]
    freqs = length // groups
    modes = lanes // (2 * freqs)
    half_lanes = lanes // 2
    half = length // 2
    pair = freqs // 2

    def kernel(
        coef_ref, modes_ref, table_ref, window_ref, out_ref, high, low, rebuilt, result, done
    ):
        lane = lax.broadcasted_iota(jnp.int32, (freqs, lanes), 1)
        row = lax.broadcasted_iota(jnp.int32, (freqs, lanes), 0)
        sign = jnp.where((row < pair) & (lane >= half_lanes), -1.0, 1.0)
        masks = [
            jnp.where((lane % half_lanes) // modes == 2 * (row % pair) + odd, sign, 0.0)
            for odd in range(2)
        ]
        for group in range(groups):
            plain = coef_ref[group]
            for kind, value in enumerate((plain, pltpu.roll(plain, half_lanes, 1))):
                rounded = value.astype(jnp.bfloat16).astype(jnp.float32)
                high[kind, group] = rounded
                low[kind, group] = value - rounded
        first = jnp.concatenate([window_ref[0]] * (columns // LANES), axis=1)
        second = jnp.concatenate([window_ref[1]] * (columns // LANES), axis=1)
        result[0] = jnp.zeros((half, columns), jnp.float32)

        def send(block):
            return pltpu.make_async_copy(result.at[block], out_ref.at[block], done.at[block])

        for group in range(groups):
            tiles = []
            for block in range(blocks):
                rows = [
                    jnp.concatenate(
                        [
                            jnp.broadcast_to(
                                side[kind, group, pl.ds(block, 1), :], (pair, lanes)
                            )
                            for kind in range(2)
                        ],
                        axis=0,
                    )
                    for side in (high, low)
                ]
                for mask in masks:
                    tiles.append(
                        jnp.concatenate(
                            [(both * mask).astype(jnp.bfloat16) for both in rows], axis=1
                        )
                    )
            values = modes_ref[group]
            product = jnp.dot(
                jnp.concatenate(tiles, axis=0),
                jnp.concatenate([values, values], axis=0),
                preferred_element_type=jnp.float32,
            )
            rebuilt[:, :, group * freqs : (group + 1) * freqs, :] = product.astype(
                jnp.bfloat16
            ).reshape(blocks, 2, freqs, columns)
        for block in range(blocks):
            even, odd = (
                jnp.dot(table_ref[i], rebuilt[block, i], preferred_element_type=jnp.float32)
                for i in range(2)
            )
            result[block] += (even + odd) * first
            result[block + 1] = (even - odd) * second
            send(block).start()
        send(blocks).start()
        for block in range(blocks + 1):
            send(block).wait()

    return pl.pallas_call(
        kernel,
        out_shape=jax.ShapeDtypeStruct((blocks + 1, half, columns), jnp.float32),
        in_specs=[pl.BlockSpec(memory_space=pltpu.VMEM)] * 4,
        out_specs=pl.BlockSpec(memory_space=pl.ANY),
        scratch_shapes=[
            pltpu.VMEM((2, groups, blocks, lanes), jnp.float32),
            pltpu.VMEM((2, groups, blocks, lanes), jnp.float32),
            pltpu.VMEM((blocks, 2, length, columns), jnp.bfloat16),
            pltpu.VMEM((blocks + 1, half, columns), jnp.float32),
            pltpu.SemaphoreType.DMA((blocks + 1,)),
        ],
        compiler_params=pltpu.CompilerParams(vmem_limit_bytes=32 * MIB),
        cost_estimate=pl.CostEstimate(
            flops=2 * length * length * blocks * columns,
            transcendentals=0,
            bytes_accessed=4 * (blocks + 1) * half * columns,
        ),
        name="synthesize",
    )(coefficients, moved_modes, table, window)


def body(spectra, eigvecs, weights):
    _, freqs, _, points_dev = spectra.shape
    groups = lax.axis_size("freq")
    factor = 1.0 / math.sqrt(points_dev * lax.axis_size("space"))
    partial, pieces = project(spectra, eigvecs, weights, groups)
    moved = lax.all_to_all(pieces, "freq", split_axis=0, concat_axis=0, tiled=True)
    copies = sum_over_space(partial, factor, groups)
    copies, moved = lax.optimization_barrier((copies, moved))
    gathered = lax.all_to_all(copies, "freq", split_axis=0, concat_axis=0, tiled=True)
    filtered = synthesize(
        gathered,
        moved.reshape(groups, -1, moved.shape[-1]),
        *transform_tables(groups * freqs, groups),
    )
    return filtered.reshape(-1, filtered.shape[-1])


def solution(mesh):
    placed = (P(None, "freq", None, "space"), P(None, "freq", None, "space"), P("space"))
    return jax.shard_map(
        body, mesh=mesh, in_specs=placed, out_specs=P(None, ("space", "freq")), check_vma=False
    )
```

```python
import math

import jax
import jax.numpy as jnp
import numpy as np
from jax import lax
from jax.experimental import pallas as pl
from jax.experimental.pallas import tpu as pltpu
from jax.sharding import PartitionSpec as P

MIB = 1024 * 1024
LANES = 128
SLAB = 4
HOPS_BY_CORE = ((0, 1), (-1, 2), (-2, -3), (4, 3))


def project(spectra, eigvecs, weights, parts):
    _, freqs, blocks, points = spectra.shape
    modes = eigvecs.shape[2]
    half = freqs * modes
    rows = 2 * freqs * blocks
    width = points // parts
    ends = [rows * (i + 1) // 4 for i in range(4)]
    starts = [0, *ends[:-1]]
    dtype = spectra.dtype

    def kernel(
        spectra_hbm, eigvecs_hbm, weights_hbm, out_ref, pieces_hbm,
        spectra_ref, eigvecs_ref, weights_ref, weighted, columns, total, pieces_ref, done, sent,
    ):
        small = pltpu.make_async_copy(weights_hbm, weights_ref, done.at[0])
        small.start()
        by_part = [
            pltpu.make_async_copy(eigvecs_hbm.at[part], eigvecs_ref.at[part], done.at[1 + part])
            for part in range(2)
        ]
        for copy in by_part:
            copy.start()
        by_rows = []
        for i, (start, end) in enumerate(zip(starts, ends)):
            some = pl.ds(start, end - start)
            by_rows.append(
                pltpu.make_async_copy(spectra_hbm.at[some], spectra_ref.at[some], done.at[3 + i])
            )
            by_rows[-1].start()
        small.wait()
        per_row = weights_ref[...].astype(jnp.float32)
        scale = jnp.concatenate([per_row[i : i + 1] for i in range(points // LANES)], axis=1)
        for part in range(2):
            by_part[part].wait()
            for k in range(freqs):
                first = part * half + k * modes
                weighted[first : first + modes] = (
                    eigvecs_ref[part, k].astype(jnp.float32) * scale
                )
        columns[...] = jnp.transpose(weighted[...].astype(dtype))
        slabs = []
        for copy, start, end in zip(by_rows, starts, ends):
            copy.wait()
            total[start:end] = jnp.dot(
                spectra_ref[start:end], columns[...], preferred_element_type=jnp.float32
            )
            if start == 0:
                for piece in range(parts):
                    pieces_ref[piece] = eigvecs_ref[:, :, :, piece * width : (piece + 1) * width]
                    if piece % SLAB == SLAB - 1:
                        some = pl.ds(piece + 1 - SLAB, SLAB)
                        slabs.append(
                            pltpu.make_async_copy(
                                pieces_ref.at[some], pieces_hbm.at[some], sent.at[len(slabs)]
                            )
                        )
                        slabs[-1].start()
        lane = lax.broadcasted_iota(jnp.int32, (blocks, 2 * half), 1)
        sums = []
        for part in range(2):
            kept = jnp.zeros((blocks, 2 * half), jnp.float32)
            for k in range(freqs):
                first = (part * freqs + k) * blocks
                own = (lane % half) // modes == k
                kept = jnp.where(own, total[first : first + blocks], kept)
            sums.append(kept)
        out_ref[...] = jnp.where(lane < half, sums[0], -sums[0]) + pltpu.roll(sums[1], half, 1)
        for copy in slabs:
            copy.wait()

    operands = (
        spectra.reshape(rows, points), eigvecs, weights.reshape(points // LANES, LANES)
    )
    return pl.pallas_call(
        kernel,
        out_shape=[
            jax.ShapeDtypeStruct((blocks, 2 * half), jnp.float32),
            jax.ShapeDtypeStruct((parts, 2, freqs, modes, width), dtype),
        ],
        in_specs=[pl.BlockSpec(memory_space=pl.ANY)] * 3,
        out_specs=[pl.BlockSpec(memory_space=pltpu.VMEM), pl.BlockSpec(memory_space=pl.ANY)],
        scratch_shapes=[
            pltpu.VMEM((rows, points), dtype),
            pltpu.VMEM(eigvecs.shape, dtype),
            pltpu.VMEM((points // LANES, LANES), dtype),
            pltpu.VMEM((2 * half, points), jnp.float32),
            pltpu.VMEM((points, 2 * half), dtype),
            pltpu.VMEM((rows, 2 * half), jnp.float32),
            pltpu.VMEM((parts, 2, freqs, modes, width), dtype),
            pltpu.SemaphoreType.DMA((3 + len(ends),)),
            pltpu.SemaphoreType.DMA((parts // SLAB,)),
        ],
        compiler_params=pltpu.CompilerParams(vmem_limit_bytes=32 * MIB),
        cost_estimate=pl.CostEstimate(
            flops=8 * freqs * blocks * modes * points,
            transcendentals=0,
            bytes_accessed=2 * (spectra.size + eigvecs.size),
        ),
        name="project",
    )(*(pltpu.with_memory_space_constraint(operand, pltpu.HBM) for operand in operands))


def gather_terms(chip, arrived, beside, factor, copies):
    def kernel(chip_ref, arrived_ref, beside_ref, out_ref):
        value = (chip_ref[...] + arrived_ref[...] + beside_ref[...]) * factor
        for copy in range(copies):
            out_ref[copy] = value

    return pl.pallas_call(
        kernel,
        out_shape=pltpu.VMEM((copies, *chip.shape), chip.dtype),
        in_specs=[pl.BlockSpec(memory_space=pltpu.VMEM)] * 3,
        out_specs=pl.BlockSpec(memory_space=pltpu.VMEM),
        compiler_params=pltpu.CompilerParams(vmem_limit_bytes=4 * MIB),
        cost_estimate=pl.CostEstimate(
            flops=3 * chip.size, transcendentals=0, bytes_accessed=4 * copies * chip.size
        ),
        name="gather_terms",
    )(chip, arrived, beside)


def sum_over_space(partial, factor, copies):
    count = lax.axis_size("space")
    chips = count // 2

    def beside(value):
        return lax.ppermute(value, "space", [(i, i ^ 1) for i in range(count)])

    def around(value, by_core):
        pairs = []
        for core, hops in enumerate(by_core):
            if hops:
                pairs += [
                    (2 * z + core, 2 * ((z + hops) % chips) + core) for z in range(chips)
                ]
        return lax.ppermute(value, "space", pairs)

    chip = partial + beside(partial)
    arrived = sum(around(chip, by_core) for by_core in HOPS_BY_CORE)
    return gather_terms(chip, arrived, beside(arrived), factor, copies)


def transform_tables(length, groups):
    freqs = length // groups
    sample = np.arange(length // 2)
    phase = 2.0 * np.pi * ((sample[:, None] * np.arange(length)[None, :]) % length) / length
    table = np.stack([np.cos(phase), -np.sin(phase)], axis=1) / math.sqrt(length)
    table = table.reshape(length // 2, 2, groups, freqs // 2, 2).transpose(4, 0, 2, 1, 3)
    window = np.sin(np.pi * (np.arange(length) + 0.5) / length).reshape(2, length // 2, 1)
    return (
        jnp.asarray(table.reshape(2, length // 2, length), jnp.bfloat16),
        jnp.asarray(np.broadcast_to(window, (2, length // 2, LANES)), jnp.float32),
    )


def synthesize(coefficients, moved_modes, table, window):
    groups, blocks, lanes = coefficients.shape
    columns = moved_modes.shape[2]
    length = table.shape[2]
    freqs = length // groups
    modes = lanes // (2 * freqs)
    half_lanes = lanes // 2
    half = length // 2
    pair = freqs // 2

    def kernel(
        coef_ref, modes_ref, table_ref, window_ref, out_ref, high, low, rebuilt, result, done
    ):
        lane = lax.broadcasted_iota(jnp.int32, (freqs, lanes), 1)
        row = lax.broadcasted_iota(jnp.int32, (freqs, lanes), 0)
        sign = jnp.where((row < pair) & (lane >= half_lanes), -1.0, 1.0)
        masks = [
            jnp.where((lane % half_lanes) // modes == 2 * (row % pair) + odd, sign, 0.0)
            for odd in range(2)
        ]
        for group in range(groups):
            plain = coef_ref[group]
            for kind, value in enumerate((plain, pltpu.roll(plain, half_lanes, 1))):
                rounded = value.astype(jnp.bfloat16).astype(jnp.float32)
                high[kind, group] = rounded
                low[kind, group] = value - rounded
        first = jnp.concatenate([window_ref[0]] * (columns // LANES), axis=1)
        second = jnp.concatenate([window_ref[1]] * (columns // LANES), axis=1)
        result[0] = jnp.zeros((half, columns), jnp.float32)

        def send(block):
            return pltpu.make_async_copy(result.at[block], out_ref.at[block], done.at[block])

        for group in range(groups):
            tiles = []
            for block in range(blocks):
                rows = [
                    jnp.concatenate(
                        [
                            jnp.broadcast_to(
                                side[kind, group, pl.ds(block, 1), :], (pair, lanes)
                            )
                            for kind in range(2)
                        ],
                        axis=0,
                    )
                    for side in (high, low)
                ]
                for mask in masks:
                    tiles.append(
                        jnp.concatenate(
                            [(both * mask).astype(jnp.bfloat16) for both in rows], axis=1
                        )
                    )
            values = modes_ref[group]
            product = jnp.dot(
                jnp.concatenate(tiles, axis=0),
                jnp.concatenate([values, values], axis=0),
                preferred_element_type=jnp.float32,
            )
            rebuilt[:, :, group * freqs : (group + 1) * freqs, :] = product.astype(
                jnp.bfloat16
            ).reshape(blocks, 2, freqs, columns)
        for block in range(blocks):
            even, odd = (
                jnp.dot(table_ref[i], rebuilt[block, i], preferred_element_type=jnp.float32)
                for i in range(2)
            )
            result[block] += (even + odd) * first
            result[block + 1] = (even - odd) * second
            send(block).start()
        send(blocks).start()
        for block in range(blocks + 1):
            send(block).wait()

    return pl.pallas_call(
        kernel,
        out_shape=jax.ShapeDtypeStruct((blocks + 1, half, columns), jnp.float32),
        in_specs=[pl.BlockSpec(memory_space=pltpu.VMEM)] * 4,
        out_specs=pl.BlockSpec(memory_space=pl.ANY),
        scratch_shapes=[
            pltpu.VMEM((2, groups, blocks, lanes), jnp.float32),
            pltpu.VMEM((2, groups, blocks, lanes), jnp.float32),
            pltpu.VMEM((blocks, 2, length, columns), jnp.bfloat16),
            pltpu.VMEM((blocks + 1, half, columns), jnp.float32),
            pltpu.SemaphoreType.DMA((blocks + 1,)),
        ],
        compiler_params=pltpu.CompilerParams(vmem_limit_bytes=32 * MIB),
        cost_estimate=pl.CostEstimate(
            flops=2 * length * length * blocks * columns,
            transcendentals=0,
            bytes_accessed=4 * (blocks + 1) * half * columns,
        ),
        name="synthesize",
    )(coefficients, moved_modes, table, window)


def body(spectra, eigvecs, weights):
    _, freqs, _, points_dev = spectra.shape
    groups = lax.axis_size("freq")
    factor = 1.0 / math.sqrt(points_dev * lax.axis_size("space"))
    partial, pieces = project(spectra, eigvecs, weights, groups)
    moved = lax.all_to_all(pieces, "freq", split_axis=0, concat_axis=0, tiled=True)
    copies = sum_over_space(partial, factor, groups)
    copies, moved = lax.optimization_barrier((copies, moved))
    gathered = lax.all_to_all(copies, "freq", split_axis=0, concat_axis=0, tiled=True)
    filtered = synthesize(
        gathered,
        moved.reshape(groups, -1, moved.shape[-1]),
        *transform_tables(groups * freqs, groups),
    )
    return filtered.reshape(-1, filtered.shape[-1])


def solution(mesh):
    placed = (P(None, "freq", None, "space"), P(None, "freq", None, "space"), P("space"))
    return jax.shard_map(
        body, mesh=mesh, in_specs=placed, out_specs=P(None, ("space", "freq")), check_vma=False
    )
```
